32 devices in a mesh: grp: 2 (over y), vel: 4 (over z), band: 4 (over x, core).
Axes of the slice: x: 2, y: 2, z: 4, core: 2. Of those that a mesh axis runs over, the one named last changes fastest.
Arguments:
- psi_image: float32 [8, 128, 512], P(('grp', 'vel'), 'band'), parts along dimension 0, may hold values from -6 to 6
- phi_image: float32 [8, 128, 512], P(('grp', 'vel'), 'band'), parts along dimension 0, may hold values from 0.5 to 4
- valid_mask: int32 [8, 128, 512], P(('grp', 'vel'), 'band'), parts along dimension 0, may hold values 0 or 1
- psf_taps: float32 [8, 21], P(('grp', 'vel')), parts along dimension 0, may hold values from 0 to 1, as said below
- shifts: int32 [64, 4, 2], P('vel'), may hold values from -16 to 16, as said below
Outputs:
- likelihood: float32 [128, 128, 512], P(('grp', 'vel'), 'band'), parts along dimension 0
The draws below stay inside these ranges and needn't reach their ends.
There are 2 independent parts, one for each index of `grp`. The reference program is written for one: setup_inputs(seed, part) draws one part's arguments, and reference() takes and returns one part's arrays. A program takes and returns all parts, laid end to end along the dimension named above; an argument that names none is the same for every part. Nothing has to cross between parts.
Inputs may be any that keep to these rules, and one draw needn't show every extreme that they name: `psf_taps`: each epoch's taps are positive and sum to one. shifts[v, e] = floor(u_v * t_e / t_last) for an integer velocity u_v of each component in -16 to 16 and non-decreasing integer epoch times t starting at 0; the first epoch's shifts are zero and the last epoch's equal u_v; both ends are reached.
All inputs are finite; a program needn't handle non-finite values. No bound on the sum of `valid_mask` on one device may be relied on, other than what follows from the above.
Results may differ from the reference program's by a relative error of at most 0.0003.
Values sent between devices are 32-bit elements; how exact they have to be, the bound alone decides.
No kernel may reach another device: no remote copies, remote signals or barrier semaphores. Data moves between devices by JAX's collectives and lax.ppermute only.
A program may use at most 64 MiB of HBM per device.

```python
import math
import jax
import jax.numpy as jnp
from jax import lax

W = 512
HALF = 10
TAPS = 21
SHIFT = 16
EPOCHS = 4
VELS = 64
H = 128


def draw_psf_taps(key, part):
    first_key, second_key = jax.random.split(key)
    sigma = jax.random.uniform(first_key, (EPOCHS, 1), jnp.float32, 1.2, 3.5)
    offsets = (jnp.arange(TAPS) - HALF).astype(jnp.float32)
    ripple = 1.0 + 0.15 * jax.random.uniform(second_key, (EPOCHS, TAPS), jnp.float32, -1.0, 1.0)
    base = jnp.exp(-offsets[None, :] ** 2 / (2.0 * sigma * sigma)) * ripple
    return base / jnp.sum(base, axis=1, keepdims=True)


def draw_shifts(key, part):
    first_key, second_key = jax.random.split(jax.random.fold_in(key, 11))
    steps = jax.random.randint(first_key, (EPOCHS - 1,), 1, 4, jnp.int32)
    times = jnp.concatenate([jnp.zeros((1,), jnp.int32), jnp.cumsum(steps).astype(jnp.int32)])
    last_time = times[EPOCHS - 1]
    velocity = jax.random.randint(second_key, (VELS, 2), -SHIFT, SHIFT + 1, jnp.int32)
    corner = jnp.array([[SHIFT, -SHIFT], [-SHIFT, SHIFT]], jnp.int32)
    velocity = velocity.at[0:2].set(corner)
    return velocity[:, None, :] * times[None, :, None] // last_time


def with_ends(entries, stream_key, least, high):
    shape = entries.shape
    index_at = [jax.random.randint(jax.random.fold_in(stream_key, axis), (), 0, shape[axis]) for axis in range(len(shape))]
    entries = entries.at[tuple(index_at)].set(least)
    longest = shape.index(max(shape))
    index_at[longest] = (index_at[longest] + 1) % shape[longest]
    return entries.at[tuple(index_at)].set(high)


def block_levels(rng, shape, shards, smallest, largest):
    loudness, own = 1.0, jax.random.fold_in(rng, 6)
    for axis_at, blocks in shards:
        steps = jnp.exp(jax.random.uniform(jax.random.fold_in(own, axis_at), (blocks,), jnp.float32, smallest / len(shards), largest / len(shards)))
        loudness = loudness * jnp.repeat(steps, shape[axis_at] // blocks).reshape([-1 if axis == axis_at else 1 for axis in range(len(shape))])
    return loudness


def gaussian(own_key, shape, scale, bound, cuts=(), kind=jnp.bfloat16):
    level = block_levels(own_key, shape, cuts, -0.22, 0.18) if cuts else 1.0
    entries = jax.random.normal(own_key, shape, jnp.float32) * scale * level
    return jnp.minimum(jnp.maximum(entries, -bound), bound).astype(kind)


def setup_inputs(seed: int = 0, part: int = 0) -> dict:
    seeds = jax.random.split(jax.random.key(seed), 6)
    part_splits = jax.random.split(jax.random.fold_in(seeds[5], part), 6)
    psi_image = gaussian(part_splits[0], (EPOCHS, H, W), 1.0, 6.0, ((0, 4), (1, 4)), jnp.float32)
    phi_image = jnp.clip(jnp.exp(math.log(4.0) - 2.0794415 * jax.random.uniform(part_splits[1], (EPOCHS, H, W), jnp.float32) ** block_levels(part_splits[1], (EPOCHS, H, W), ((0, 4), (1, 4)), -0.2, 0.2)), 0.5, 4.0)
    valid_mask = with_ends((jax.random.randint(part_splits[2], (EPOCHS, H, W), 0, 8) < 7).astype(jnp.int32), jax.random.fold_in(part_splits[2], 1), 0, 1)
    psf_taps = draw_psf_taps(jax.random.fold_in(jax.random.fold_in(seeds[5], part), 71), part)
    shifts = draw_shifts(jax.random.fold_in(seeds[5], 71), part)
    return dict(psi_image=psi_image, phi_image=phi_image, valid_mask=valid_mask, psf_taps=psf_taps, shifts=shifts)


phi_floor = 0.1

def col_filter(stacked, kernels):
    half_width = (kernels.shape[2] - 1) // 2
    width = stacked.shape[3]
    padded = jnp.pad(stacked, ((0, 0), (0, 0), (0, 0), (half_width, half_width)))
    total = jnp.zeros(stacked.shape, jnp.float32)
    for offset in range(kernels.shape[2]):
        total = total + kernels[:, :, offset, None, None] * padded[:, :, :, offset:offset + width]
    return total

def row_filter(extended, kernels, rows_out):
    total = jnp.zeros(extended.shape[:2] + (rows_out, extended.shape[3]), jnp.float32)
    for offset in range(kernels.shape[2]):
        total = total + kernels[:, :, offset, None, None] * extended[:, :, offset:offset + rows_out, :]
    return total

def reference(psi_image, phi_image, valid_mask, psf_taps, shifts):
    weight = valid_mask.astype(jnp.float32)
    stacked = jnp.stack([psi_image * weight, phi_image * weight], axis=1)
    kernels = jnp.stack([psf_taps, psf_taps * psf_taps], axis=1)
    col_done = col_filter(stacked, kernels)
    extended = jnp.pad(col_done, ((0, 0), (0, 0), (HALF, HALF), (0, 0)))
    filtered = row_filter(extended, kernels, H)
    padded = jnp.pad(filtered, ((0, 0), (0, 0), (SHIFT, SHIFT), (SHIFT, SHIFT)))

    def one_velocity(velocity_shifts):

        def one_epoch(image, pair):
            anchor = jnp.zeros((), jnp.int32)
            return lax.dynamic_slice(image, (anchor, (pair[0] + SHIFT).astype(jnp.int32), (pair[1] + SHIFT).astype(jnp.int32)), (2, H, W))
        pieces = jax.vmap(one_epoch)(padded, velocity_shifts)
        totals = lax.optimization_barrier(jnp.sum(pieces, axis=0))
        return totals[0] / jnp.sqrt(jnp.maximum(totals[1], phi_floor))
    return lax.map(one_velocity, shifts)
```

```python
import functools
import jax
import jax.numpy as jnp
from jax import lax
from jax.experimental import pallas as pl
from jax.experimental.pallas import tpu as pltpu
from jax.sharding import PartitionSpec as P

phi_floor = 0.1
LANES = 128
SUB = 8
VMEM = pltpu.VMEM
SMEM = pltpu.SMEM


def spec(space):
    return pl.BlockSpec(memory_space=space)


def partner_pairs(count, step):
    if count & (count - 1) == 0:
        return [(i, i ^ step) for i in range(count)]
    return [(i, (i + step) % count) for i in range(count)]


def partner_of(index, count, step):
    if count & (count - 1) == 0:
        return index ^ step
    return lax.rem(index + (count - step), count)


def pack_kernel(psi_ref, phi_ref, mask_ref, taps_ref, out_ref, *, rows, blocks, taps, half):
    margin = LANES // 2
    for c in range(blocks):
        lanes = slice(c * LANES, (c + 1) * LANES)
        weight = mask_ref[0, :, lanes].astype(jnp.float32)
        out_ref[c * rows:(c + 1) * rows, :] = psi_ref[0, :, lanes] * weight
        out_ref[(blocks + c) * rows:(blocks + c + 1) * rows, :] = phi_ref[0, :, lanes] * weight
    lane = lax.broadcasted_iota(jnp.int32, (1, LANES), 1)
    forward = jnp.zeros((1, LANES), jnp.float32)
    reverse = jnp.zeros((1, LANES), jnp.float32)
    for j in range(taps):
        value = taps_ref[0:1, j:j + 1]
        forward = jnp.where(lane == j, value, forward)
        reverse = jnp.where(lane == margin + half - j, value, reverse)
    last = 2 * blocks * rows
    out_ref[last:last + SUB, :] = jnp.concatenate(
        [forward, reverse, jnp.zeros((SUB - 2, LANES), jnp.float32)], axis=0)


def split(value):
    high = value.astype(jnp.bfloat16)
    return high, (value - high.astype(jnp.float32)).astype(jnp.bfloat16)


def filter_epoch(own, low, high, ext, store, slot, top, bottom, *, rows, blocks, taps, half, shift):
    margin = LANES // 2
    wide = rows + 2 * shift
    last = 2 * blocks * rows
    for image in range(2):
        for c in range(blocks):
            k = image * blocks + c
            piece = slice(k * rows, (k + 1) * rows)
            ext[k, 0:rows, :] = low[piece, :]
            ext[k, rows:2 * rows, :] = own[piece, :]
            ext[k, 2 * rows:3 * rows, :] = high[piece, :]
    row = lax.broadcasted_iota(jnp.int32, (wide, LANES), 0)
    lane = lax.broadcasted_iota(jnp.int32, (wide, LANES), 1)
    inside = jnp.logical_and(row >= top, row < bottom)
    for image in range(2):
        forward = own[last:last + 1, :]
        reverse = own[last + 1:last + 2, :]
        if image:
            forward = forward * forward
            reverse = reverse * reverse
        coefs = [jnp.broadcast_to(forward[:, i:i + 1], (SUB, LANES)) for i in range(taps)]
        highs, lows = [], []
        for c in range(blocks):
            k = image * blocks + c
            parts = []
            for t in range(wide // SUB):
                total = None
                for i in range(taps):
                    start = rows - shift - half + t * SUB + i
                    term = ext[k, start:start + SUB, :] * coefs[i]
                    total = term if total is None else total + term
                parts.append(total)
            block_high, block_low = split(jnp.concatenate(parts, axis=0))
            highs.append(block_high)
            lows.append(block_low)
        base = jnp.concatenate(
            [jnp.broadcast_to(reverse, (LANES, LANES)), jnp.zeros((LANES, LANES), jnp.float32)], axis=1)
        toeplitz = pltpu.roll(base, 0, 1, stride=1, stride_axis=0)
        t_high, t_low = split(toeplitz)
        b_high = jnp.concatenate(highs, axis=0)
        b_low = jnp.concatenate(lows, axis=0)
        both = jnp.dot(b_high, t_high, preferred_element_type=jnp.float32)
        both += jnp.dot(b_low, t_high, preferred_element_type=jnp.float32)
        both += jnp.dot(b_high, t_low, preferred_element_type=jnp.float32)
        for k in range(blocks + 1):
            keep = inside
            if k == 0:
                value = both[0:wide, 0:LANES]
                keep = jnp.logical_and(keep, lane >= margin)
            elif k == blocks:
                value = both[(k - 1) * wide:k * wide, LANES:2 * LANES]
                keep = jnp.logical_and(keep, lane < margin)
            else:
                value = both[k * wide:(k + 1) * wide, 0:LANES] + both[(k - 1) * wide:k * wide, LANES:2 * LANES]
            store[slot, image, k] = jnp.where(keep, value, 0.0)


def stack_velocity(shifts_ref, store, v, order, *, rows, blocks, shift):
    margin = LANES // 2
    lane = lax.broadcasted_iota(jnp.int32, (rows, LANES), 1)
    totals = [[None] * blocks for _ in range(2)]
    for slot, epoch in enumerate(order):
        start = shifts_ref[v, 2 * epoch] + shift
        turn = LANES - margin - shifts_ref[v, 2 * epoch + 1]
        for image in range(2):
            turned = [
                pltpu.roll(store[slot, image, k, pl.ds(start, rows), :], turn, 1)
                for k in range(blocks + 1)
            ]
            for c in range(blocks):
                piece = jnp.where(lane < turn, turned[c], turned[c + 1])
                old = totals[image][c]
                totals[image][c] = piece if old is None else old + piece
    return totals


def search_kernel(shifts_ref, *refs, count, rows, blocks, taps, half, shift, bands):
    owns, cores, crosses = refs[:count], refs[count:2 * count], refs[2 * count:3 * count]
    out_ref, store, ext, stage, sems = refs[3 * count:]
    band = lax.axis_index("band")
    here = lax.axis_index("vel")
    velocities = shifts_ref.shape[0]
    wide = rows + 2 * shift
    top = jnp.where(band == 0, shift, 0)
    bottom = jnp.where(band == bands - 1, shift + rows, wide)
    sizes = dict(rows=rows, blocks=blocks, taps=taps, half=half, shift=shift)

    for parity in range(2):
        @pl.when(lax.rem(band, 2) == parity)
        def _():
            for slot in range(count):
                low, high = (crosses, cores) if parity == 0 else (cores, crosses)
                filter_epoch(owns[slot], low[slot], high[slot], ext, store, slot, top, bottom, **sizes)

    order = [here] + [partner_of(here, count, step) for step in range(1, count)]

    def body(v, carry):
        totals = stack_velocity(shifts_ref, store, v, order, rows=rows, blocks=blocks, shift=shift)
        for c in range(blocks):
            value = totals[0][c] / jnp.sqrt(jnp.maximum(totals[1][c], phi_floor))
            stage[v, :, c * LANES:(c + 1) * LANES] = value
        pltpu.make_async_copy(stage.at[v], out_ref.at[v], sems.at[v]).start()
        return carry

    lax.fori_loop(0, velocities, body, 0)
    for v in range(velocities):
        pltpu.make_async_copy(stage.at[v], out_ref.at[v], sems.at[v]).wait()


def local(psi_image, phi_image, valid_mask, psf_taps, shifts, *, count, bands):
    rows = psi_image.shape[1]
    width = psi_image.shape[2]
    taps = psf_taps.shape[1]
    half = (taps - 1) // 2
    shift = rows // 2
    blocks = width // LANES
    velocities = shifts.shape[0]
    wide = rows + 2 * shift
    packed_rows = 2 * blocks * rows + SUB
    packed = jax.ShapeDtypeStruct((packed_rows, LANES), jnp.float32)
    own = pl.pallas_call(
        functools.partial(pack_kernel, rows=rows, blocks=blocks, taps=taps, half=half),
        out_shape=packed,
        in_specs=[spec(VMEM)] * 4,
        out_specs=spec(VMEM),
        name="pack",
    )(psi_image, phi_image, valid_mask, psf_taps)
    owns = [own] + [lax.ppermute(own, "vel", partner_pairs(count, step)) for step in range(1, count)]
    core_pairs = [(b, b ^ 1) for b in range(bands) if b ^ 1 < bands]
    cross_pairs = [(b, (b + 1 ^ 1) - 1) for b in range(bands) if 0 <= (b + 1 ^ 1) - 1 < bands]
    cores = [lax.ppermute(block, "band", core_pairs) for block in owns]
    crosses = [lax.ppermute(block, "band", cross_pairs) for block in owns]
    return pl.pallas_call(
        functools.partial(search_kernel, count=count, rows=rows, blocks=blocks, taps=taps, half=half,
                          shift=shift, bands=bands),
        out_shape=jax.ShapeDtypeStruct((velocities, rows, width), jnp.float32),
        in_specs=[spec(SMEM)] + [spec(VMEM)] * (3 * count),
        out_specs=spec(pl.ANY),
        scratch_shapes=[
            VMEM((count, 2, blocks + 1, wide, LANES), jnp.float32),
            VMEM((2 * blocks, 3 * rows, LANES), jnp.float32),
            VMEM((velocities, rows, width), jnp.float32),
            pltpu.SemaphoreType.DMA((velocities,)),
        ],
        name="search",
    )(shifts.reshape(velocities, -1), *owns, *cores, *crosses)


def solution(mesh):
    sizes = dict(mesh.shape)
    placed = (
        P(("grp", "vel"), "band", None),
        P(("grp", "vel"), "band", None),
        P(("grp", "vel"), "band", None),
        P(("grp", "vel"), None),
        P("vel", None, None),
    )
    return jax.shard_map(
        functools.partial(local, count=sizes["vel"], bands=sizes["band"]),
        mesh=mesh,
        in_specs=placed,
        out_specs=P(("grp", "vel"), "band", None),
        check_vma=False,
    )
```

```python
import functools
import jax
import jax.numpy as jnp
from jax import lax
from jax.experimental import pallas as pl
from jax.experimental.pallas import tpu as pltpu
from jax.sharding import PartitionSpec as P


phi_floor = 0.1
LANES = 128
SUB = 8
VMEM = pltpu.VMEM
SMEM = pltpu.SMEM


def spec(space):
    return pl.BlockSpec(memory_space=space)


def source_step(step):
    return step & (step - 1)


def step_pairs(count, step):
    hop = step & -step
    return [(i, i ^ hop) for i in range(count)]


def core_pairs(bands):
    return [(b, b ^ 1) for b in range(bands)]


def cross_pairs(bands):
    return [(b, (b + 2) % bands if b % 2 == 0 else (b - 2) % bands) for b in range(bands)]


def in_vmem(x):
    return pltpu.with_memory_space_constraint(x, VMEM)


def pack_kernel(psi_hbm, phi_hbm, mask_hbm, taps_hbm, out_ref, psi_ref, phi_ref, mask_ref, taps_ref, sems,
                *, rows, blocks, taps, half, first):
    margin = LANES // 2
    copies = [
        pltpu.make_async_copy(source, target, sems.at[i])
        for i, (source, target) in enumerate(
            ((psi_hbm, psi_ref), (mask_hbm, mask_ref), (phi_hbm, phi_ref), (taps_hbm, taps_ref)))
    ]
    for copy in copies:
        copy.start()
    for copy in copies:
        copy.wait()
    for c in range(blocks):
        lanes = slice(c * LANES, (c + 1) * LANES)
        weight = mask_ref[0, :, lanes].astype(jnp.float32)
        out_ref[c * rows:(c + 1) * rows, :] = psi_ref[0, :, lanes] * weight
        out_ref[(blocks + c) * rows:(blocks + c + 1) * rows, :] = phi_ref[0, :, lanes] * weight
    lane = lax.broadcasted_iota(jnp.int32, (1, LANES), 1)
    forward = jnp.zeros((1, LANES), jnp.float32)
    reverse = jnp.zeros((1, LANES), jnp.float32)
    for j in range(taps):
        value = taps_ref[0:1, j:j + 1]
        forward = jnp.where(lane == first + j, value, forward)
        reverse = jnp.where(lane == margin + half - j, value, reverse)
    last = 2 * blocks * rows
    out_ref[last:last + SUB, :] = jnp.concatenate(
        [forward, reverse, jnp.zeros((SUB - 2, LANES), jnp.float32)], axis=0)


def split(value):
    high = value.astype(jnp.bfloat16)
    return high, (value - high.astype(jnp.float32)).astype(jnp.bfloat16)


def matmul3(a_high, a_low, b_high, b_low, twice_b):
    if twice_b:
        both = jnp.dot(jnp.concatenate([a_high, a_low], axis=1), jnp.concatenate([b_high, b_high], axis=0),
                       preferred_element_type=jnp.float32)
        return both + jnp.dot(a_high, b_low, preferred_element_type=jnp.float32)
    both = jnp.dot(jnp.concatenate([a_high, a_high], axis=1), jnp.concatenate([b_high, b_low], axis=0),
                   preferred_element_type=jnp.float32)
    return both + jnp.dot(a_low, b_high, preferred_element_type=jnp.float32)


def trim_kernel(core, out_ref, *, rows, blocks, reach):
    start = jnp.where(lax.rem(lax.axis_index("band"), 2) == 0, rows - reach, 0)
    for k in range(2 * blocks):
        out_ref[k * reach:(k + 1) * reach, :] = core[pl.ds(k * rows + start, reach), :]


def half_kernel(own, core, out_ref, *, rows, blocks, reach):
    band = lax.axis_index("band")
    start = jnp.where(band < 2, rows - reach, 0)
    inner = jnp.logical_or(band == 1, band == 2)
    for source, image, mine in ((own, 0, True), (core, 1, False)):
        @pl.when(inner == mine)
        def _():
            for c in range(blocks):
                at = pl.ds((image * blocks + c) * rows + start, reach)
                out_ref[c * reach:(c + 1) * reach, :] = source[at, :]


def join_kernel(own, half, out_ref, *, rows, blocks, reach):
    start = jnp.where(lax.rem(lax.axis_index("band"), 2) == 0, rows - reach, 0)
    for k in range(2 * blocks):
        out_ref[k * reach:(k + 1) * reach, :] = own[pl.ds(k * rows + start, reach), :]
    out_ref[2 * blocks * reach:, :] = half[...]


def neighbour_rows(halo, parity, k, edge, *, rows, blocks, reach):
    kind, refs = halo
    if kind == "joined":
        joined, _ = refs
        beside = joined[k * reach:(k + 1) * reach, :]
    else:
        start = k * rows + (0 if parity == 0 else rows - reach)
        beside = refs[0][start:start + reach, :]
    if kind == "line":
        across = refs[1][k * reach:(k + 1) * reach, :]
    elif k >= blocks:
        across = refs[-1][(k - blocks) * reach:(k - blocks + 1) * reach, :]
    elif kind == "joined":
        across = joined[(2 * blocks + k) * reach:(2 * blocks + k + 1) * reach, :]
    else:
        across = refs[1][k * reach:(k + 1) * reach, :]
    return beside, jnp.where(edge, 0.0, across)


def filter_into(own, halo, ext, store, band, *, rows, blocks, taps, half, shift, bands):
    margin = LANES // 2
    wide = rows + 2 * shift
    reach = half + shift
    last = 2 * blocks * rows
    top = jnp.where(band == 0, shift, 0)
    bottom = jnp.where(band == bands - 1, shift + rows, wide)
    edge = jnp.logical_or(band == 0, band == bands - 1)
    for parity in range(2):
        @pl.when(lax.rem(band, 2) == parity)
        def _():
            for k in range(2 * blocks):
                beside, across = neighbour_rows(halo, parity, k, edge, rows=rows, blocks=blocks, reach=reach)
                low, high = (across, beside) if parity == 0 else (beside, across)
                ext[k, 0:rows - reach, :] = jnp.zeros((rows - reach, LANES), jnp.float32)
                ext[k, rows - reach:rows, :] = low
                ext[k, 2 * rows:2 * rows + reach, :] = high
                ext[k, 2 * rows + reach:3 * rows, :] = jnp.zeros((rows - reach, LANES), jnp.float32)
    for k in range(2 * blocks):
        ext[k, rows:2 * rows, :] = own[k * rows:(k + 1) * rows, :]
    row = lax.broadcasted_iota(jnp.int32, (wide, LANES), 0)
    lane = lax.broadcasted_iota(jnp.int32, (wide, LANES), 1)
    banded = pltpu.roll(jnp.broadcast_to(own[last:last + 1, :], (wide, LANES)), 0, 1, stride=1, stride_axis=0)
    banded = jnp.where(jnp.logical_and(row >= top, row < bottom), banded, 0.0)
    base = jnp.concatenate([jnp.broadcast_to(own[last + 1:last + 2, :], (LANES, LANES)),
                            jnp.zeros((LANES, LANES), jnp.float32)], axis=1)
    toeplitz = pltpu.roll(base, 0, 1, stride=1, stride_axis=0)
    for image in range(2):
        if image:
            banded, toeplitz = banded * banded, toeplitz * toeplitz
        r_high, r_low = split(banded)
        below = jnp.zeros((LANES - 3 * rows, blocks * LANES), jnp.bfloat16)
        e_high, e_low = [
            jnp.concatenate([part, below], axis=0)
            for part in split(jnp.concatenate([ext[image * blocks + c] for c in range(blocks)], axis=1))
        ]
        done = matmul3(r_high, r_low, e_high, e_low, False)
        t_high, t_low = split(toeplitz)
        b_high, b_low = split(jnp.concatenate([done[:, c * LANES:(c + 1) * LANES] for c in range(blocks)], axis=0))
        both = matmul3(b_high, b_low, t_high, t_low, True)
        for k in range(blocks):
            value = both[k * wide:(k + 1) * wide, 0:LANES]
            left = both[((k - 1) % blocks) * wide:((k - 1) % blocks + 1) * wide, LANES:2 * LANES]
            value = jnp.where(lane >= margin, value, left) if k == 0 else value + left
            store[image, k] = value


def shifted_epoch(store, row_shift, column_shift, use, *, rows, blocks, shift):
    margin = LANES // 2
    lane = lax.broadcasted_iota(jnp.int32, (SUB, LANES), 1)
    start = row_shift + shift
    turn = LANES - margin - column_shift
    mask = lane < turn
    first = jnp.logical_and(mask, lane >= turn - margin)
    past = lane >= turn + margin
    for t in range(rows // SUB):
        for image in range(2):
            turned = [
                pltpu.roll(store[image, k, pl.ds(start + t * SUB, SUB), :], turn, 1)
                for k in range(blocks)
            ]
            pieces = []
            for c in range(blocks):
                here, after = turned[c], turned[(c + 1) % blocks]
                if c == 0:
                    here = jnp.where(first, here, 0.0)
                if c == blocks - 1:
                    after = jnp.where(past, 0.0, after)
                pieces.append(jnp.where(mask, here, after))
            use(t, image, pieces)


def every_velocity(shifts, store, base, epoch, velocities, use, end=None, *, most, rows, blocks, shift):
    places = dict(rows=rows, blocks=blocks, shift=shift)

    @pl.when(epoch == 0)
    def _():
        def keep(t, image, pieces):
            for c in range(blocks):
                base[t, image, c] = pieces[c]

        shifted_epoch(store, 0, 0, keep, **places)

        def one_velocity(v):
            for t in range(rows // SUB):
                for image in range(2):
                    use(v, t, image, [base[t, image, c] for c in range(blocks)])
            if end:
                end(v)

        each_velocity(velocities, one_velocity, most)

    @pl.when(epoch != 0)
    def _():
        def one_velocity(v):
            shifted_epoch(store, shifts[epoch, 0, v], shifts[epoch, 1, v], functools.partial(use, v), **places)
            if end:
                end(v)

        each_velocity(velocities, one_velocity, most)


def each_velocity(velocities, one_velocity, most):
    unroll = most
    while velocities % unroll:
        unroll //= 2

    def body(i, carry):
        for u in range(unroll):
            one_velocity(i * unroll + u)
        return carry

    lax.fori_loop(0, velocities // unroll, body, 0)


def epoch_kernel(shifts_ref, own, *refs, step, kind, parts, **sizes):
    halo, totals, (total_ref, store, ext, base, shifts, sem) = (kind, refs[:parts]), refs[parts:-6], refs[-6:]
    rows, blocks, shift = sizes["rows"], sizes["blocks"], sizes["shift"]
    copy = pltpu.make_async_copy(shifts_ref, shifts, sem)
    copy.start()
    filter_into(own, halo, ext, store, lax.axis_index("band"), **sizes)
    copy.wait()

    def use(v, t, image, pieces):
        for c in range(blocks):
            piece = totals[0][v, image, t, c] + pieces[c] if totals else pieces[c]
            total_ref[v, image, t, c] = piece

    every_velocity(shifts, store, base, lax.axis_index("vel") ^ step, total_ref.shape[0], use,
                   most=16, rows=rows, blocks=blocks, shift=shift)


def last_kernel(shifts_ref, own, *refs, step, kind, parts, **sizes):
    halo, (total_ref, out_ref, store, ext, base, shifts, sem, stage, sems) = (kind, refs[:parts]), refs[parts:]
    rows, blocks, shift = sizes["rows"], sizes["blocks"], sizes["shift"]
    velocities = total_ref.shape[0]
    copy = pltpu.make_async_copy(shifts_ref, shifts, sem)
    copy.start()
    filter_into(own, halo, ext, store, lax.axis_index("band"), **sizes)
    copy.wait()
    psi = {}

    def use(v, t, image, pieces):
        for c in range(blocks):
            total = total_ref[v, image, t, c] + pieces[c]
            if image == 0:
                psi[c] = total
            else:
                value = psi[c] * lax.rsqrt(jnp.maximum(total, phi_floor))
                stage[v, t * SUB:(t + 1) * SUB, c * LANES:(c + 1) * LANES] = value

    def end(v):
        pltpu.make_async_copy(stage.at[v], out_ref.at[v], sems.at[v]).start()

    every_velocity(shifts, store, base, lax.axis_index("vel") ^ step, velocities, use, end,
                   most=16, rows=rows, blocks=blocks, shift=shift)
    for v in range(velocities):
        pltpu.make_async_copy(stage.at[v], out_ref.at[v], sems.at[v]).wait()


def local(psi_image, phi_image, valid_mask, psf_taps, shifts, *, count, bands):
    rows = psi_image.shape[1]
    width = psi_image.shape[2]
    taps = psf_taps.shape[1]
    half = (taps - 1) // 2
    shift = rows // 2
    blocks = width // LANES
    velocities = shifts.shape[0]
    wide = rows + 2 * shift
    packed_rows = 2 * blocks * rows + SUB
    packed = jax.ShapeDtypeStruct((packed_rows, LANES), jnp.float32)
    in_hbm = [pltpu.with_memory_space_constraint(x, pltpu.HBM) for x in (psi_image, phi_image, valid_mask, psf_taps)]
    own = pl.pallas_call(
        functools.partial(pack_kernel, rows=rows, blocks=blocks, taps=taps, half=half, first=rows - shift - half),
        out_shape=packed,
        in_specs=[spec(pl.ANY)] * 4,
        out_specs=spec(VMEM),
        scratch_shapes=[VMEM(x.shape, x.dtype) for x in in_hbm] + [pltpu.SemaphoreType.DMA((4,))],
        compiler_params=pltpu.CompilerParams(vmem_limit_bytes=4 << 20),
        name="pack",
    )(*in_hbm)
    owns = [own]
    for step in range(1, count):
        owns.append(lax.ppermute(owns[source_step(step)], "vel", step_pairs(count, step)))
    sizes = dict(rows=rows, blocks=blocks, taps=taps, half=half, shift=shift, bands=bands)
    filtered = (2, blocks, wide, LANES)
    reach = half + shift
    summed = jax.ShapeDtypeStruct((velocities, 2, rows // SUB, blocks, SUB, LANES), jnp.float32)
    total_bytes = summed.size * 4
    ext = VMEM((2 * blocks, 3 * rows, LANES), jnp.float32)
    shifts = pltpu.with_memory_space_constraint(jnp.transpose(shifts, (1, 2, 0)), pltpu.HBM)
    in_smem = SMEM(shifts.shape, shifts.dtype)

    def place(kernel, out_rows, *operands):
        return pl.pallas_call(
            functools.partial(kernel, rows=rows, blocks=blocks, reach=reach),
            out_shape=jax.ShapeDtypeStruct((out_rows, LANES), jnp.float32),
            in_specs=[spec(VMEM)] * len(operands),
            out_specs=spec(VMEM),
            compiler_params=pltpu.CompilerParams(vmem_limit_bytes=2 << 20),
        )(*[in_vmem(x) for x in operands])

    paired = bands == 4
    halves = {}
    totals = []
    for step in (0, 2, 1, 3) if count == 4 and paired else range(count):
        block = owns[step]
        if paired:
            if step == 0:
                core = lax.ppermute(block, "band", core_pairs(bands))
                half_rows = place(half_kernel, blocks * reach, block, core)
                halves[step] = lax.ppermute(half_rows, "band", [(b, b ^ 2) for b in range(bands)])
                beside = lax.ppermute(halves[step], "band", core_pairs(bands))
                kind, parts = "first", (core, beside, halves[step])
            else:
                halves[step] = lax.ppermute(halves[source_step(step)], "vel", step_pairs(count, step))
                joined = place(join_kernel, 3 * blocks * reach, block, halves[step])
                kind, parts = "joined", (lax.ppermute(joined, "band", core_pairs(bands)), halves[step])
        else:
            core = lax.ppermute(block, "band", core_pairs(bands))
            trimmed = place(trim_kernel, 2 * blocks * reach, core)
            kind, parts = "line", (core, lax.ppermute(trimmed, "band", cross_pairs(bands)))
        operands = (shifts, *[in_vmem(x) for x in (block, *parts, *totals)])
        in_specs = [spec(pl.ANY)] + [spec(VMEM)] * (len(operands) - 1)
        sem = pltpu.SemaphoreType.DMA
        base = VMEM((rows // SUB, 2, blocks, SUB, LANES), jnp.float32)
        scratch = [VMEM(filtered, jnp.float32), ext, base, in_smem, sem]
        if step < count - 1:
            totals = [pl.pallas_call(
                functools.partial(epoch_kernel, step=step, kind=kind, parts=len(parts), **sizes),
                out_shape=summed,
                in_specs=in_specs,
                out_specs=spec(VMEM),
                scratch_shapes=scratch,
                compiler_params=pltpu.CompilerParams(vmem_limit_bytes=(6 << 20) + 2 * total_bytes),
                name="epoch",
            )(*operands)]
    return pl.pallas_call(
        functools.partial(last_kernel, step=count - 1, kind=kind, parts=len(parts), **sizes),
        out_shape=jax.ShapeDtypeStruct((velocities, rows, width), jnp.float32),
        in_specs=in_specs,
        out_specs=spec(pl.ANY),
        scratch_shapes=scratch + [VMEM((velocities, rows, width), jnp.float32), sem((velocities,))],
        compiler_params=pltpu.CompilerParams(vmem_limit_bytes=(6 << 20) + 2 * total_bytes),
        name="last",
    )(*operands)


def solution(mesh):
    sizes = dict(mesh.shape)
    assert sizes["vel"] & (sizes["vel"] - 1) == 0 and sizes["band"] % 2 == 0
    placed = (
        P(("grp", "vel"), "band", None),
        P(("grp", "vel"), "band", None),
        P(("grp", "vel"), "band", None),
        P(("grp", "vel"), None),
        P("vel", None, None),
    )
    count = sizes["vel"]

    def body(*args):
        return local(*args, count=count, bands=sizes["band"])

    return jax.shard_map(
        body,
        mesh=mesh,
        in_specs=placed,
        out_specs=P(("grp", "vel"), "band", None),
        check_vma=False,
    )
```
